32 devices in a mesh: grp: 4 (over y, x), seq: 8 (over z, core).
Axes of the slice: x: 2, y: 2, z: 4, core: 2. Of those that a mesh axis runs over, the one named last changes fastest.
Arguments:
- tokens: bfloat16 [4096, 2048], P(('grp', 'seq')), may hold values from -6.6 to 6.6
- grad_output: bfloat16 [4096, 2048], P(('grp', 'seq')), may hold values from -6 to 6
- query_gain: float32 [2048], replicated, may hold values from -6 to 6
- key_gain: float32 [2048], replicated, may hold values from -6 to 6
- short_query_gain: float32 [2048], replicated, may hold values from -24 to 24
- short_key_gain: float32 [2048], replicated, may hold values from -24 to 24
Outputs:
- grad_tokens: bfloat16 [4096, 2048], P(('grp', 'seq'))
- gain_grads: float32 [4, 2048], replicated
The draws below stay inside these ranges and needn't reach their ends.
All inputs are finite; a program needn't handle non-finite values.
Results may differ from the reference program's by a relative error of at most 0.019.
Values may be sent and summed in bfloat16 or wider, within the bound.
No kernel may reach another device: no remote copies, remote signals or barrier semaphores. Data moves between devices by JAX's collectives and lax.ppermute only.
A program may use at most 64 MiB of HBM per device.

```python
import jax
import jax.numpy as jnp
from jax import lax

D = 2048
HEADS = 16
TOK_DEV = 128
WINDOW = 128
SHORTEN = 16
TOKENS = 4096


def draw_tokens(key, part):
    values = jnp.clip(jax.random.normal(jax.random.fold_in(key, 1), (TOKENS, D), jnp.float32), -6.0, 6.0)
    return values.astype(jnp.bfloat16)


def gain_draw(key, salt, spread):
    values = spread * jnp.clip(jax.random.normal(jax.random.fold_in(key, salt), (D,), jnp.float32), -6.0, 6.0)
    return values.astype(jnp.float32)


def draw_query_gain(key, part):
    return gain_draw(key, 3, 1.0)


def draw_key_gain(key, part):
    return gain_draw(key, 4, 1.0)


def draw_short_query_gain(key, part):
    return gain_draw(key, 5, 4.0)


def draw_short_key_gain(key, part):
    return gain_draw(key, 6, 4.0)


def levels(stream_key, extent, pieces, least, high):
    loudness = 1.0
    for position, blocks in pieces:
        draws = jax.random.uniform(jax.random.fold_in(jax.random.fold_in(stream_key, 6), position), (blocks,), jnp.float32, least / len(pieces), high / len(pieces))
        loudness = loudness * jnp.repeat(jnp.exp(draws), extent[position] // blocks).reshape((-1,) + (1,) * (len(extent) - 1 - position))
    return loudness


def noise(key, dims, scale, reach, pieces=(), kind=jnp.bfloat16):
    values = jax.random.normal(key, dims, jnp.float32) * scale
    if len(pieces) > 0:
        values = levels(key, dims, pieces, -0.22, 0.18) * values
    return jnp.clip(values, min=-reach, max=reach).astype(kind)


def setup_inputs(seed: int = 0) -> dict:
    key_of = jax.random.split(jax.random.key(seed), 7)
    return {
        "tokens": draw_tokens(jax.random.fold_in(key_of[6], 71), 0),
        "grad_output": noise(key_of[1], (TOKENS, D), 1.0, 6.0, ((0, 32),)),
        "query_gain": draw_query_gain(jax.random.fold_in(key_of[6], 71), 0),
        "key_gain": draw_key_gain(jax.random.fold_in(key_of[6], 71), 0),
        "short_query_gain": draw_short_query_gain(jax.random.fold_in(key_of[6], 71), 0),
        "short_key_gain": draw_short_key_gain(jax.random.fold_in(key_of[6], 71), 0),
    }


def rounded(values):
    return lax.optimization_barrier(values.astype(jnp.bfloat16)).astype(jnp.float32)


def attention_weights(queries, key_rows, allowed):
    temper = queries.shape[-1] ** -0.5
    scores = jnp.einsum("qhe,khe->hqk", queries.astype(jnp.float32), key_rows.astype(jnp.float32)) * temper
    scores = jnp.where(allowed[None], scores, -1e30)
    log_total = jax.nn.logsumexp(scores, axis=-1)
    return jnp.where(allowed[None], jnp.exp(scores - log_total[..., None]), 0.0)


def attention_output(queries, key_rows, value_rows, allowed):
    weights = attention_weights(queries, key_rows, allowed)
    return jnp.einsum("hqk,khe->qhe", rounded(weights), value_rows.astype(jnp.float32))


def attention_grads(queries, key_rows, value_rows, incoming, allowed):
    temper = queries.shape[-1] ** -0.5
    weights = attention_weights(queries, key_rows, allowed)
    incoming_f = incoming.astype(jnp.float32)
    grad_weights = jnp.einsum("qhe,khe->hqk", incoming_f, value_rows.astype(jnp.float32))
    row_dot = jnp.sum(weights * grad_weights, axis=-1, keepdims=True)
    grad_scores = rounded(weights * (grad_weights - row_dot))
    grad_queries = jnp.einsum("hqk,khe->qhe", grad_scores, key_rows.astype(jnp.float32)) * temper
    grad_keys = jnp.einsum("hqk,qhe->khe", grad_scores, queries.astype(jnp.float32)) * temper
    grad_values = jnp.einsum("hqk,qhe->khe", rounded(weights), incoming_f)
    return grad_queries, grad_keys, grad_values


def reference(tokens, grad_output, query_gain, key_gain, short_query_gain, short_key_gain):
    length = tokens.shape[0]
    model_width = tokens.shape[1]
    head_size = model_width // HEADS
    blocks = length // TOK_DEV
    token_f = tokens.astype(jnp.float32)
    query_heads = (token_f * query_gain).astype(jnp.bfloat16).reshape(length, HEADS, head_size)
    key_heads = (token_f * key_gain).astype(jnp.bfloat16).reshape(length, HEADS, head_size)
    value_heads = tokens.reshape(length, HEADS, head_size)
    padding = jnp.zeros((WINDOW, HEADS, head_size), jnp.bfloat16)
    keys_padded = jnp.concatenate([padding, key_heads], axis=0)
    values_padded = jnp.concatenate([padding, value_heads], axis=0)

    def local_allowed(base):
        query_pos = base + jnp.arange(TOK_DEV, dtype=jnp.int32)[:, None]
        key_pos = base - WINDOW + jnp.arange(TOK_DEV + WINDOW, dtype=jnp.int32)[None, :]
        return (key_pos <= query_pos) & (key_pos > query_pos - WINDOW) & (key_pos >= 0)

    def block_inputs(block):
        base = (block * TOK_DEV).astype(jnp.int32)
        queries = lax.dynamic_slice_in_dim(query_heads, base, TOK_DEV, 0)
        key_rows = lax.dynamic_slice_in_dim(keys_padded, base, TOK_DEV + WINDOW, 0)
        value_rows = lax.dynamic_slice_in_dim(values_padded, base, TOK_DEV + WINDOW, 0)
        return base, queries, key_rows, value_rows

    def forward_block(block):
        base, queries, key_rows, value_rows = block_inputs(block)
        return attention_output(queries, key_rows, value_rows, local_allowed(base))

    starts = jnp.arange(blocks, dtype=jnp.int32)
    local_out = lax.map(forward_block, starts).reshape(length, model_width)
    mixed_rows = (token_f + local_out).astype(jnp.bfloat16)
    shifted = jnp.concatenate([jnp.zeros((SHORTEN - 1, model_width), jnp.bfloat16), mixed_rows], axis=0)[:length]
    short_len = length // SHORTEN
    pooled = (shifted.astype(jnp.float32).reshape(short_len, SHORTEN, model_width).sum(axis=1) * (1.0 / SHORTEN)).astype(jnp.bfloat16)
    grad_short = grad_output.astype(jnp.float32).reshape(short_len, SHORTEN, model_width).sum(axis=1).astype(jnp.bfloat16)
    pooled_f = pooled.astype(jnp.float32)
    short_queries = (pooled_f * short_query_gain).astype(jnp.bfloat16).reshape(short_len, HEADS, head_size)
    short_keys = (pooled_f * short_key_gain).astype(jnp.bfloat16).reshape(short_len, HEADS, head_size)
    short_values = pooled.reshape(short_len, HEADS, head_size)
    short_incoming = grad_short.reshape(short_len, HEADS, head_size)
    causal = jnp.arange(short_len, dtype=jnp.int32)[:, None] >= jnp.arange(short_len, dtype=jnp.int32)[None, :]

    def short_head(inputs):
        queries, key_rows, value_rows, incoming = inputs
        grads = attention_grads(queries[:, None], key_rows[:, None], value_rows[:, None], incoming[:, None], causal)
        return grads[0][:, 0], grads[1][:, 0], grads[2][:, 0]

    def by_head(values):
        return jnp.transpose(values, (1, 0, 2))

    def by_row(values):
        return jnp.transpose(values, (1, 0, 2)).reshape(short_len, model_width)

    short_gq, short_gk, short_gv = lax.map(short_head, (by_head(short_queries), by_head(short_keys), by_head(short_values), by_head(short_incoming)))
    short_gq = by_row(short_gq)
    short_gk = by_row(short_gk)
    short_gv = by_row(short_gv)
    grad_pooled = grad_short.astype(jnp.float32) + short_gq * short_query_gain + short_gk * short_key_gain + short_gv
    grad_short_query = jnp.sum(short_gq * pooled_f, axis=0)
    grad_short_key = jnp.sum(short_gk * pooled_f, axis=0)
    grad_following = jnp.concatenate([grad_pooled[1:], jnp.zeros((1, model_width), jnp.float32)], axis=0)
    spread = jnp.concatenate([grad_pooled[:, None], jnp.broadcast_to(grad_following[:, None], (short_len, SHORTEN - 1, model_width))], axis=1) * (1.0 / SHORTEN)
    grad_mixed = grad_output.astype(jnp.float32) + spread.reshape(length, model_width)
    incoming_heads = grad_mixed.astype(jnp.bfloat16).reshape(length, HEADS, head_size)

    def backward_block(block):
        base, queries, key_rows, value_rows = block_inputs(block)
        incoming = lax.dynamic_slice_in_dim(incoming_heads, base, TOK_DEV, 0)
        return attention_grads(queries, key_rows, value_rows, incoming, local_allowed(base))

    local_gq, local_gk, local_gv = lax.map(backward_block, starts)

    def settle(grads):
        own_rows = grads[:, WINDOW:]
        carried = jnp.concatenate([grads[1:, :WINDOW], jnp.zeros_like(grads[:1, :WINDOW])], axis=0)
        own_rows = own_rows.at[:, TOK_DEV - WINDOW:].add(carried)
        return own_rows.reshape(length, model_width)

    local_gq = local_gq.reshape(length, model_width)
    local_gk = settle(local_gk)
    local_gv = settle(local_gv)
    grad_tokens = (grad_mixed + local_gq * query_gain + local_gk * key_gain + local_gv).astype(jnp.bfloat16)
    gain_grads = jnp.stack([jnp.sum(local_gq * token_f, axis=0), jnp.sum(local_gk * token_f, axis=0), grad_short_query, grad_short_key]) * (length ** -0.5)
    return grad_tokens, gain_grads.astype(jnp.float32)
```

```python
import functools

import jax
import jax.numpy as jnp
from jax import lax
from jax.experimental import pallas as pl
from jax.experimental.pallas import tpu as pltpu
from jax.sharding import PartitionSpec as P

HEADS = 16
WINDOW = 128
SHORTEN = 16


NEGATIVE = -1e30
CHAIN = ("grp", "seq")
TILE = 8
COPIES = 2


def shifted_2(value, axis, steps):
    count = lax.axis_size(axis)
    leading, last = (max(0, -steps), min(count, count - steps))
    return lax.ppermute(value, axis, [(source, source + steps) for source in range(leading, last)])


def mm(a, b):
    return lax.dot_general(a, b, (((1,), (0,)), ((), ())), preferred_element_type=jnp.float32)


def mm_nt(a, b):
    return lax.dot_general(a, b, (((1,), (1,)), ((), ())), preferred_element_type=jnp.float32)


def mm_tn(a, b):
    return lax.dot_general(a, b, (((0,), (0,)), ((), ())), preferred_element_type=jnp.float32)


def iotas(rows, columns):
    return (
        lax.broadcasted_iota(jnp.int32, (rows, columns), 0),
        lax.broadcasted_iota(jnp.int32, (rows, columns), 1),
    )


def chain_index():
    return lax.axis_index("grp") * lax.axis_size("seq") + lax.axis_index("seq")


def own_kernel(tokens, grad_output, gains, out, peak, total, grad_short):
    rows, width = tokens.shape
    size = width // HEADS
    temper = size ** (-0.5)
    q_pos, k_pos = iotas(rows, rows)
    allowed = k_pos <= q_pos
    short, row = iotas(rows // SHORTEN, rows)
    pool = (row // SHORTEN == short).astype(jnp.bfloat16)
    lane = lax.broadcasted_iota(jnp.int32, (rows, size), 1)
    peaks = jnp.zeros((rows, size), jnp.float32)
    totals = jnp.zeros((rows, size), jnp.float32)
    for head in range(HEADS):
        part = slice(head * size, (head + 1) * size)
        low = tokens[:, part]
        x = low.astype(jnp.float32)
        q = (x * gains[0:1, part]).astype(jnp.bfloat16)
        k = (x * gains[1:2, part]).astype(jnp.bfloat16)
        scores = jnp.where(allowed, mm_nt(q, k) * temper, NEGATIVE)
        high = jnp.max(scores, axis=1, keepdims=True)
        weights = jnp.exp(scores - high)
        out[:, part] = mm(weights.astype(jnp.bfloat16), low)
        peaks = jnp.where(lane == head, high, peaks)
        totals = jnp.where(lane == head, jnp.sum(weights, axis=1, keepdims=True), totals)
        grad_short[head] = mm(pool, grad_output[:, part]).astype(jnp.bfloat16)
    peak[...] = peaks
    total[...] = totals


def prior_kernel(tokens, prior, gains, out, peak, total, grad_short, send):
    rows, width = tokens.shape
    size = width // HEADS
    temper = size ** (-0.5)
    q_pos, k_pos = iotas(rows, rows)
    allowed = (k_pos > q_pos) & (chain_index() > 0)
    short, row = iotas(2 * TILE, rows)
    pool = ((row + SHORTEN - 1) // SHORTEN == short).astype(jnp.bfloat16)
    tile_row = lax.broadcasted_iota(jnp.int32, (TILE, size), 0)
    for head in range(HEADS):
        part = slice(head * size, (head + 1) * size)
        x = tokens[:, part].astype(jnp.float32)
        low = prior[:, part]
        q = (x * gains[0:1, part]).astype(jnp.bfloat16)
        k = (low.astype(jnp.float32) * gains[1:2, part]).astype(jnp.bfloat16)
        scores = jnp.where(allowed, mm_nt(q, k) * temper, NEGATIVE)
        own_high = peak[:, head : head + 1]
        high = jnp.maximum(jnp.max(scores, axis=1, keepdims=True), own_high)
        weights = jnp.exp(scores - high)
        fade = jnp.exp(own_high - high)
        sums = total[:, head : head + 1] * fade + jnp.sum(weights, axis=1, keepdims=True)
        local = (out[:, part] * fade + mm(weights.astype(jnp.bfloat16), low)) / sums
        mixed = (x + local).astype(jnp.bfloat16)
        pooled = mm(pool, mixed)
        rows_sent = jnp.where(tile_row == 0, pooled[:TILE], pooled[:TILE] * (1.0 / SHORTEN))
        tail = pooled[TILE:]
        tail_high = tail.astype(jnp.bfloat16).astype(jnp.float32)
        tail_low = pltpu.roll(tail - tail_high, 1, 0)
        tail_rows = jnp.where(tile_row == 0, tail_high, tail_low)
        for copy in range(COPIES):
            send[head * COPIES + copy, 0:TILE, :] = rows_sent.astype(jnp.bfloat16)
            send[head * COPIES + copy, TILE : 2 * TILE, :] = tail_rows.astype(jnp.bfloat16)
            send[head * COPIES + copy, 2 * TILE : 3 * TILE, :] = grad_short[head]


def short_kernel(received, gains, send):
    count, _, size = received.shape
    rows = count * TILE
    temper = size ** (-0.5)
    me = chain_index()
    head = me // COPIES
    copy = me % COPIES
    gain_q = gains[pl.ds(head, 1), :]
    gain_k = gains[pl.ds(HEADS + head, 1), :]
    tile_row = lax.broadcasted_iota(jnp.int32, (count, TILE, size), 1)
    tails = received[:, TILE : 2 * TILE, :].astype(jnp.float32)
    tails = tails[:, 0:1, :] + tails[:, 1:2, :]
    tails = jnp.concatenate([jnp.zeros((1, 1, size), jnp.float32), tails[:-1]], axis=0)
    pooled = received[:, 0:TILE, :].astype(jnp.float32)
    pooled = jnp.where(tile_row == 0, (pooled + tails) * (1.0 / SHORTEN), pooled)
    values = pooled.reshape(rows, size).astype(jnp.bfloat16)
    pooled = values.astype(jnp.float32)
    q = (pooled * gain_q).astype(jnp.bfloat16)
    k = (pooled * gain_k).astype(jnp.bfloat16)
    incoming_f = received[:, 2 * TILE : 3 * TILE, :].astype(jnp.float32).reshape(rows, size)
    incoming = incoming_f.astype(jnp.bfloat16)
    q_pos, k_pos = iotas(rows, rows)
    scores = jnp.where(k_pos <= q_pos, mm_nt(q, k) * temper, NEGATIVE)
    weights = jnp.exp(scores - jnp.max(scores, axis=1, keepdims=True))
    weights = weights / jnp.sum(weights, axis=1, keepdims=True)
    grads = mm_nt(incoming, values)
    dots = jnp.sum(weights * grads, axis=1, keepdims=True)
    ds = (weights * (grads - dots)).astype(jnp.bfloat16)
    grad_q = mm(ds, k) * temper
    grad_k = mm_tn(ds, q) * temper
    grad_v = mm_tn(weights.astype(jnp.bfloat16), incoming)
    grad = incoming_f + grad_q * gain_q + grad_k * gain_k + grad_v
    sum_q = jnp.sum(grad_q * pooled, axis=0, keepdims=True)
    sum_k = jnp.sum(grad_k * pooled, axis=0, keepdims=True)
    gain = jnp.where(copy == 0, sum_q, sum_k)
    gain_high = gain.astype(jnp.bfloat16).astype(jnp.float32)
    gain_low = gain - gain_high
    half = TILE // COPIES
    grad = grad.reshape(count, TILE, size)
    following = jnp.concatenate([grad[1:, 0:1, :], jnp.zeros((1, 1, size), jnp.float32)], axis=0)
    later = jnp.where(tile_row == half, following, jnp.roll(grad, -half, axis=1))
    block = jnp.where(copy == 0, grad, later)
    block = jnp.where(tile_row == half + 1, gain_high[None], block)
    block = jnp.where(tile_row == half + 2, gain_low[None], block)
    block = jnp.where(tile_row == half + 3, 0.0, block)
    send[...] = block.astype(jnp.bfloat16)


def backward_kernel(tokens, prior, grad_output, gains, received, returned, partial, send, sums):
    rows, width = tokens.shape
    size = width // HEADS
    temper = size ** (-0.5)
    half = TILE // COPIES
    q_pos, k_pos = iotas(rows, rows)
    own_allowed = k_pos <= q_pos
    prior_allowed = (k_pos > q_pos) & (chain_index() > 0)
    row, column = iotas(rows, 2 * TILE)
    short = (row + SHORTEN - 1) // SHORTEN
    short = jnp.where(short > half, short + (TILE - half), short)
    spread = (short == column).astype(jnp.bfloat16)
    for head in range(HEADS):
        part = slice(head * size, (head + 1) * size)
        gain_q, gain_k = gains[0:1, part], gains[1:2, part]
        own = tokens[:, part]
        before = prior[:, part]
        x = own.astype(jnp.float32)
        x_before = before.astype(jnp.float32)
        q = (x * gain_q).astype(jnp.bfloat16)
        k = (x * gain_k).astype(jnp.bfloat16)
        k_before = (x_before * gain_k).astype(jnp.bfloat16)
        own_scores = jnp.where(own_allowed, mm_nt(q, k) * temper, NEGATIVE)
        prior_scores = jnp.where(prior_allowed, mm_nt(q, k_before) * temper, NEGATIVE)
        high = jnp.maximum(
            jnp.max(own_scores, axis=1, keepdims=True), jnp.max(prior_scores, axis=1, keepdims=True)
        )
        own_w = jnp.exp(own_scores - high)
        prior_w = jnp.exp(prior_scores - high)
        inverse = 1.0 / (
            jnp.sum(own_w, axis=1, keepdims=True) + jnp.sum(prior_w, axis=1, keepdims=True)
        )
        own_w = own_w * inverse
        prior_w = prior_w * inverse
        grad_pooled = received[head * COPIES : (head + 1) * COPIES].reshape(2 * TILE, size)
        grad_mixed = grad_output[:, part].astype(jnp.float32) + mm(spread, grad_pooled) * (
            1.0 / SHORTEN
        )
        incoming = grad_mixed.astype(jnp.bfloat16)
        own_dw = mm_nt(incoming, own)
        prior_dw = mm_nt(incoming, before)
        dots = jnp.sum(own_w * own_dw + prior_w * prior_dw, axis=1, keepdims=True)
        own_ds = (own_w * (own_dw - dots)).astype(jnp.bfloat16)
        prior_ds = (prior_w * (prior_dw - dots)).astype(jnp.bfloat16)
        grad_q = (mm(own_ds, k) + mm(prior_ds, k_before)) * temper
        own_gk = mm_tn(own_ds, q) * temper
        prior_gk = mm_tn(prior_ds, q) * temper
        own_gv = mm_tn(own_w.astype(jnp.bfloat16), incoming)
        prior_gv = mm_tn(prior_w.astype(jnp.bfloat16), incoming)
        returned[:, part] = (prior_gk * gain_k + prior_gv).astype(jnp.bfloat16)
        partial[:, part] = grad_mixed + grad_q * gain_q + own_gk * gain_k + own_gv
        sums[head : head + 1, :] = jnp.sum(grad_q * x, axis=0, keepdims=True)
        sums[HEADS + head : HEADS + head + 1, :] = jnp.sum(
            own_gk * x + prior_gk * x_before, axis=0, keepdims=True
        )
    block = sums[...].astype(jnp.bfloat16)
    for device in range(send.shape[0]):
        send[device] = block


def final_kernel(partial, arriving, received, short, grad_tokens, gain_grads, *, scale):
    size = received.shape[-1]
    half = TILE // COPIES
    grad_tokens[...] = (partial[...] + arriving[...].astype(jnp.float32)).astype(jnp.bfloat16)
    sums = jnp.sum(received[...].astype(jnp.float32), axis=0) * scale
    for head in range(HEADS):
        part = slice(head * size, (head + 1) * size)
        gain_grads[0:1, part] = sums[head : head + 1]
        gain_grads[1:2, part] = sums[HEADS + head : HEADS + head + 1]
        for copy in range(COPIES):
            block = short[head * COPIES + copy].astype(jnp.float32)
            total = block[half + 1 : half + 2] + block[half + 2 : half + 3]
            gain_grads[2 + copy : 3 + copy, part] = total * scale


def call(kernel, outputs, flops, scratch=()):
    return pl.pallas_call(
        kernel,
        out_shape=outputs,
        scratch_shapes=list(scratch),
        cost_estimate=pl.CostEstimate(flops=flops, bytes_accessed=1 << 20, transcendentals=1 << 19),
    )


def exchange(value):
    return lax.all_to_all(value, CHAIN, split_axis=0, concat_axis=0, tiled=True)


def head_shards(tokens, grad_output, query_gain, key_gain, short_query_gain, short_key_gain):
    rows, width = tokens.shape
    size = width // HEADS
    count = lax.axis_size(CHAIN)
    array = jax.ShapeDtypeStruct
    low, full = jnp.bfloat16, jnp.float32
    product = 2 * rows * rows * width
    gains = jnp.stack([query_gain, key_gain])
    short_gains = jnp.stack([short_query_gain, short_key_gain]).reshape(2 * HEADS, size)
    prior = shifted_2(tokens, CHAIN, 1)
    own_out, peak, total, grad_short = call(
        own_kernel,
        [
            array((rows, width), full),
            array((rows, size), full),
            array((rows, size), full),
            array((HEADS, rows // SHORTEN, size), low),
        ],
        2 * product,
    )(tokens, grad_output, gains)
    send = call(prior_kernel, array((count, 3 * TILE, size), low), 2 * product)(
        tokens, prior, gains, own_out, peak, total, grad_short
    )
    back = call(short_kernel, array((count, TILE, size), low), 10 * (count * TILE) ** 2 * size)(
        exchange(send), short_gains
    )
    back = exchange(back)
    returned, partial, sums = call(
        backward_kernel,
        [
            array((rows, width), low),
            array((rows, width), full),
            array((count, 2 * HEADS, size), low),
        ],
        10 * product,
        [pltpu.VMEM((2 * HEADS, size), full)],
    )(tokens, prior, grad_output, gains, back)
    arriving = shifted_2(returned, CHAIN, -1)
    sums = exchange(sums)
    return call(
        functools.partial(final_kernel, scale=(rows * count) ** (-0.5)),
        [array((rows, width), low), array((4, width), full)],
        0,
    )(partial, arriving, sums, back)


def head_scores(queries, key_rows):
    temper = queries.shape[-1] ** (-0.5)
    return (
        jnp.einsum("qhe,khe->hqk", queries, key_rows, preferred_element_type=jnp.float32) * temper
    )


def short_order(absolute, block_rows, group_rows, seq_count):
    within = absolute % group_rows
    source = absolute // group_rows
    return (within // block_rows * seq_count + source) * block_rows + within % block_rows


def shards(tokens, grad_output, query_gain, key_gain, short_query_gain, short_key_gain):
    local_rows, model_width = tokens.shape
    head_size = model_width // HEADS
    temper = head_size ** (-0.5)
    chain_index = lax.axis_index(("grp", "seq"))
    token_f = tokens.astype(jnp.float32)
    query_heads = (token_f * query_gain).astype(jnp.bfloat16).reshape(local_rows, HEADS, head_size)
    prior_rows = shifted_2(tokens, ("grp", "seq"), 1)
    context = jnp.concatenate([prior_rows, tokens], axis=0)
    context_f = context.astype(jnp.float32)
    key_heads = (
        (context_f * key_gain).astype(jnp.bfloat16).reshape(local_rows + WINDOW, HEADS, head_size)
    )
    value_heads = context.reshape(local_rows + WINDOW, HEADS, head_size)
    query_pos = chain_index * local_rows + jnp.arange(local_rows, dtype=jnp.int32)[:, None]
    key_pos = (
        chain_index * local_rows
        - WINDOW
        + jnp.arange(local_rows + WINDOW, dtype=jnp.int32)[None, :]
    )
    allowed = (key_pos <= query_pos) & (key_pos > query_pos - WINDOW) & (key_pos >= 0)
    scores = jnp.where(allowed[None], head_scores(query_heads, key_heads), NEGATIVE)
    log_total = jax.nn.logsumexp(scores, axis=-1)
    weights = jnp.where(allowed[None], jnp.exp(scores - log_total[..., None]), 0.0)
    weights_low = weights.astype(jnp.bfloat16)
    local_out = jnp.einsum(
        "hqk,khe->qhe", weights_low, value_heads, preferred_element_type=jnp.float32
    ).reshape(local_rows, model_width)
    mixed_rows = (token_f + local_out).astype(jnp.bfloat16)
    tail_rows = shifted_2(mixed_rows[local_rows - (SHORTEN - 1) :], ("grp", "seq"), 1)
    shifted = jnp.concatenate([tail_rows, mixed_rows], axis=0)[:local_rows]
    short_rows = local_rows // SHORTEN
    pooled = (
        shifted.astype(jnp.float32).reshape(short_rows, SHORTEN, model_width).sum(axis=1)
        * (1.0 / SHORTEN)
    ).astype(jnp.bfloat16)
    grad_short = (
        grad_output.astype(jnp.float32)
        .reshape(short_rows, SHORTEN, model_width)
        .sum(axis=1)
        .astype(jnp.bfloat16)
    )
    groups = lax.axis_size("grp")
    seq_count = lax.axis_size("seq")
    group_index = lax.axis_index("grp")
    seq_index = lax.axis_index("seq")
    head_width = model_width // groups
    head_part = head_width // head_size
    group_rows = short_rows * groups
    pooled_here, grad_here = (
        lax.all_to_all(
            pooled.reshape(short_rows, groups, head_width),
            "grp",
            split_axis=1,
            concat_axis=0,
            tiled=True,
        ),
        lax.all_to_all(
            grad_short.reshape(short_rows, groups, head_width),
            "grp",
            split_axis=1,
            concat_axis=0,
            tiled=True,
        ),
    )
    pooled_here = pooled_here.reshape(group_rows, head_width)
    grad_here = grad_here.reshape(group_rows, head_width)
    gain_query = lax.dynamic_slice_in_dim(short_query_gain, group_index * head_width, head_width)
    gain_key = lax.dynamic_slice_in_dim(short_key_gain, group_index * head_width, head_width)
    pooled_f = pooled_here.astype(jnp.float32)
    short_queries = (
        (pooled_f * gain_query).astype(jnp.bfloat16).reshape(group_rows, head_part, head_size)
    )
    short_keys = (
        (pooled_f * gain_key).astype(jnp.bfloat16).reshape(group_rows, head_part, head_size)
    )
    short_values = pooled_here.reshape(group_rows, head_part, head_size)
    short_incoming = grad_here.reshape(group_rows, head_part, head_size)
    own_pos = short_order(
        seq_index * group_rows + jnp.arange(group_rows, dtype=jnp.int32),
        short_rows,
        group_rows,
        seq_count,
    )
    peak = jnp.full((head_part, group_rows), NEGATIVE, jnp.float32)
    fetched_keys = lax.all_gather(short_keys, "seq", axis=0, tiled=True)
    fetched_values = lax.all_gather(short_values, "seq", axis=0, tiled=True)
    remote_pos = short_order(
        jnp.arange(fetched_keys.shape[0], dtype=jnp.int32), short_rows, group_rows, seq_count
    )
    visible = remote_pos[None, :] <= own_pos[:, None]
    piece_scores = jnp.where(visible[None], head_scores(short_queries, fetched_keys), NEGATIVE)
    highest = jnp.maximum(peak, piece_scores.max(axis=-1))
    piece_weights = jnp.where(visible[None], jnp.exp(piece_scores - highest[..., None]), 0.0)
    piece_grads = jnp.einsum(
        "qhe,khe->hqk", short_incoming, fetched_values, preferred_element_type=jnp.float32
    )
    total_sum = piece_weights.sum(axis=-1)
    weighted_sum = (piece_weights * piece_grads).sum(axis=-1)
    short_log_total = highest + jnp.log(total_sum)
    short_dot = weighted_sum / total_sum
    fetched_keys = lax.all_gather(short_keys, "seq", axis=0, tiled=True)
    fetched_values = lax.all_gather(short_values, "seq", axis=0, tiled=True)
    remote_pos = short_order(
        jnp.arange(fetched_keys.shape[0], dtype=jnp.int32), short_rows, group_rows, seq_count
    )
    visible = remote_pos[None, :] <= own_pos[:, None]
    piece_weights = jnp.where(
        visible[None],
        jnp.exp(head_scores(short_queries, fetched_keys) - short_log_total[..., None]),
        0.0,
    )
    piece_grads = jnp.einsum(
        "qhe,khe->hqk", short_incoming, fetched_values, preferred_element_type=jnp.float32
    )
    piece_ds = (piece_weights * (piece_grads - short_dot[..., None])).astype(jnp.bfloat16)
    short_gq = (
        jnp.einsum("hqk,khe->qhe", piece_ds, fetched_keys, preferred_element_type=jnp.float32)
        * temper
    )
    stats_all, dots_all = (
        lax.all_gather(short_log_total.T, "seq", axis=0, tiled=True),
        lax.all_gather(short_dot.T, "seq", axis=0, tiled=True),
    )
    fetched_queries = lax.all_gather(short_queries, "seq", axis=0, tiled=True)
    fetched_incoming = lax.all_gather(short_incoming, "seq", axis=0, tiled=True)
    count = fetched_queries.shape[0]
    remote_pos = short_order(jnp.arange(count, dtype=jnp.int32), short_rows, group_rows, seq_count)
    visible = own_pos[None, :] <= remote_pos[:, None]
    remote_total = stats_all.T
    remote_dot = dots_all.T
    piece_weights = jnp.where(
        visible[None],
        jnp.exp(head_scores(fetched_queries, short_keys) - remote_total[..., None]),
        0.0,
    )
    piece_grads = jnp.einsum(
        "qhe,khe->hqk", fetched_incoming, short_values, preferred_element_type=jnp.float32
    )
    piece_ds = (piece_weights * (piece_grads - remote_dot[..., None])).astype(jnp.bfloat16)
    grad_keys = (
        jnp.einsum("hqk,qhe->khe", piece_ds, fetched_queries, preferred_element_type=jnp.float32)
        * temper
    )
    grad_values = jnp.einsum(
        "hqk,qhe->khe",
        piece_weights.astype(jnp.bfloat16),
        fetched_incoming,
        preferred_element_type=jnp.float32,
    )
    short_gk = grad_keys
    short_gv = grad_values
    short_gq = short_gq.reshape(group_rows, head_width)
    short_gk = short_gk.reshape(group_rows, head_width)
    short_gv = short_gv.reshape(group_rows, head_width)
    grad_pooled_here = (
        grad_here.astype(jnp.float32) + short_gq * gain_query + short_gk * gain_key + short_gv
    )
    empty_width = jnp.zeros((model_width,), jnp.float32)
    grad_short_query = lax.dynamic_update_slice(
        empty_width, jnp.sum(short_gq * pooled_f, axis=0), (group_index * head_width,)
    )
    grad_short_key = lax.dynamic_update_slice(
        empty_width, jnp.sum(short_gk * pooled_f, axis=0), (group_index * head_width,)
    )
    grad_pooled = (
        lax.all_to_all(
            grad_pooled_here.reshape(group_rows, 1, head_width).astype(jnp.bfloat16),
            "grp",
            split_axis=0,
            concat_axis=1,
            tiled=True,
        )
        .astype(jnp.float32)
        .reshape(short_rows, model_width)
    )
    following = shifted_2(grad_pooled[:1], ("grp", "seq"), -1)
    grad_following = jnp.concatenate([grad_pooled[1:], following], axis=0)
    spread = jnp.concatenate(
        [
            grad_pooled[:, None],
            jnp.broadcast_to(grad_following[:, None], (short_rows, SHORTEN - 1, model_width)),
        ],
        axis=1,
    ) * (1.0 / SHORTEN)
    grad_mixed = grad_output.astype(jnp.float32) + spread.reshape(local_rows, model_width)
    incoming_heads = grad_mixed.astype(jnp.bfloat16).reshape(local_rows, HEADS, head_size)
    local_dw = jnp.einsum(
        "qhe,khe->hqk", incoming_heads, value_heads, preferred_element_type=jnp.float32
    )
    local_dot = jnp.sum(weights * local_dw, axis=-1, keepdims=True)
    local_ds = (weights * (local_dw - local_dot)).astype(jnp.bfloat16)
    local_gq = (
        jnp.einsum("hqk,khe->qhe", local_ds, key_heads, preferred_element_type=jnp.float32) * temper
    ).reshape(local_rows, model_width)
    full_gk = (
        jnp.einsum("hqk,qhe->khe", local_ds, query_heads, preferred_element_type=jnp.float32)
        * temper
    ).reshape(local_rows + WINDOW, model_width)
    full_gv = jnp.einsum(
        "hqk,qhe->khe", weights_low, incoming_heads, preferred_element_type=jnp.float32
    ).reshape(local_rows + WINDOW, model_width)
    returned = full_gk[:WINDOW] * key_gain + full_gv[:WINDOW]
    arriving = shifted_2(returned.astype(jnp.bfloat16), ("grp", "seq"), -1).astype(returned.dtype)
    edge_gain = jnp.sum(full_gk[:WINDOW] * context_f[:WINDOW], axis=0)
    local_gk = full_gk[WINDOW:]
    local_gv = full_gv[WINDOW:]
    grad_tokens = grad_mixed + local_gq * query_gain + local_gk * key_gain + local_gv
    grad_tokens = grad_tokens.at[local_rows - WINDOW :].add(arriving)
    grad_query_gain = jnp.sum(local_gq * token_f, axis=0)
    grad_key_gain = jnp.sum(local_gk * token_f, axis=0) + edge_gain
    summed = lax.psum(
        jnp.stack([grad_query_gain, grad_key_gain, grad_short_query, grad_short_key]),
        ("grp", "seq"),
    )
    total_tokens = local_rows * lax.axis_size(("grp", "seq"))
    return (grad_tokens.astype(jnp.bfloat16), summed * total_tokens ** (-0.5))


def solution(mesh):
    paired = mesh.size == COPIES * HEADS
    return jax.shard_map(
        head_shards if paired else shards,
        mesh=mesh,
        in_specs=(P(("grp", "seq"), None), P(("grp", "seq"), None), P(), P(), P(), P()),
        out_specs=(P(("grp", "seq"), None), P()),
        check_vma=False,
    )
```

```python
import functools

import jax
import jax.numpy as jnp
from jax import lax
from jax.experimental import pallas as pl
from jax.experimental.pallas import tpu as pltpu
from jax.sharding import PartitionSpec as P

HEADS = 16
WINDOW = 128
SHORTEN = 16


NEGATIVE = -1e30
LOG2_E = 1.4426950408889634
CHAIN = ("grp", "seq")
TILE = 8
COPIES = 2


def shifted_2(value, axis, steps):
    count = lax.axis_size(axis)
    leading, last = (max(0, -steps), min(count, count - steps))
    return lax.ppermute(value, axis, [(source, source + steps) for source in range(leading, last)])


def mm(a, b):
    return lax.dot_general(a, b, (((1,), (0,)), ((), ())), preferred_element_type=jnp.float32)


def mm_nt(a, b):
    return lax.dot_general(a, b, (((1,), (1,)), ((), ())), preferred_element_type=jnp.float32)


def mm_tn(a, b):
    return lax.dot_general(a, b, (((0,), (0,)), ((), ())), preferred_element_type=jnp.float32)


def iotas(rows, columns):
    return (
        lax.broadcasted_iota(jnp.int32, (rows, columns), 0),
        lax.broadcasted_iota(jnp.int32, (rows, columns), 1),
    )


def chain_index():
    return lax.axis_index("grp") * lax.axis_size("seq") + lax.axis_index("seq")


def staggered(work):
    active = []
    waiting = list(range(HEADS))
    while waiting or active:
        if waiting:
            active.append(work(waiting.pop(0)))
        active = [item for item in active if next(item, True) is None]


def raised(scores, high, size):
    return jnp.exp2((scores - high) * (size ** (-0.5) * LOG2_E))


def own_kernel(
    tokens, grad_output, query_gain, key_gain, weights, peak, total, queries, grad_short
):
    rows, width = tokens.shape
    size = width // HEADS
    k_pos, q_pos = iotas(rows, rows)
    allowed = k_pos <= q_pos
    short, row = iotas(rows // SHORTEN, rows)
    pool = (row // SHORTEN == short).astype(jnp.bfloat16)

    def work(head):
        part = slice(head * size, (head + 1) * size)
        x = tokens[:, part].astype(jnp.float32)
        q = (x * query_gain[:, part]).astype(jnp.bfloat16)
        k = (x * key_gain[:, part]).astype(jnp.bfloat16)
        queries[:, part] = q
        scores = jnp.where(allowed, mm_nt(k, q), NEGATIVE)
        grad_short[head] = mm(pool, grad_output[:, part]).astype(jnp.bfloat16)
        yield
        high = jnp.max(scores, axis=0, keepdims=True)
        peak[head : head + 1, :] = high
        yield
        own = raised(scores, high, size)
        weights[head] = own
        total[head : head + 1, :] = jnp.sum(own, axis=0, keepdims=True)

    staggered(work)


def prior_kernel(
    tokens, prior, key_gain, queries, own_weights, peak, total, grad_short, send, weights
):
    rows, width = tokens.shape
    size = width // HEADS
    k_pos, q_pos = iotas(rows, rows)
    allowed = (k_pos > q_pos) & (chain_index() > 0)
    short, row = iotas(2 * TILE, rows)
    pool = ((row + SHORTEN - 1) // SHORTEN == short).astype(jnp.bfloat16)
    tile_row = lax.broadcasted_iota(jnp.int32, (TILE, size), 0)

    def work(head):
        part = slice(head * size, (head + 1) * size)
        before = prior[:, part]
        k = (before.astype(jnp.float32) * key_gain[:, part]).astype(jnp.bfloat16)
        scores = jnp.where(allowed, mm_nt(k, queries[:, part]), NEGATIVE)
        yield
        own_high = peak[head : head + 1, :]
        high = jnp.maximum(jnp.max(scores, axis=0, keepdims=True), own_high)
        yield
        prior_w = raised(scores, high, size)
        fade = raised(own_high, high, size)
        scale = 1.0 / (jnp.sum(prior_w, axis=0, keepdims=True) + total[head : head + 1, :] * fade)
        yield
        both = jnp.concatenate(
            [
                (prior_w * scale).astype(jnp.bfloat16),
                (own_weights[head] * (fade * scale)).astype(jnp.bfloat16),
            ],
            axis=0,
        )
        weights[head] = both
        own = tokens[:, part]
        local = mm_tn(both, jnp.concatenate([before, own], axis=0))
        yield
        mixed = (own.astype(jnp.float32) + local).astype(jnp.bfloat16)
        pooled = mm(pool, mixed)
        yield
        rows_sent = jnp.where(tile_row == 0, pooled[:TILE], pooled[:TILE] * (1.0 / SHORTEN))
        tail = pooled[TILE:]
        tail_high = tail.astype(jnp.bfloat16).astype(jnp.float32)
        tail_low = pltpu.roll(tail - tail_high, 1, 0)
        tail_rows = jnp.where(tile_row == 0, tail_high, tail_low)
        for copy in range(COPIES):
            send[head * COPIES + copy, 0:TILE, :] = rows_sent.astype(jnp.bfloat16)
            send[head * COPIES + copy, TILE : 2 * TILE, :] = tail_rows.astype(jnp.bfloat16)
            send[head * COPIES + copy, 2 * TILE : 3 * TILE, :] = grad_short[head]

    staggered(work)


def short_kernel(received, query_gain, key_gain, send):
    count, _, size = received.shape
    rows = count * TILE
    temper = size ** (-0.5)
    me = chain_index()
    copy = me % COPIES
    part = pl.ds(pl.multiple_of(me // COPIES * size, size), size)
    gain_q, gain_k = query_gain[:, part], key_gain[:, part]
    tile_row = lax.broadcasted_iota(jnp.int32, (count, TILE, size), 1)
    tails = received[:, TILE : 2 * TILE, :].astype(jnp.float32)
    tails = tails[:, 0:1, :] + tails[:, 1:2, :]
    tails = jnp.concatenate([jnp.zeros((1, 1, size), jnp.float32), tails[:-1]], axis=0)
    pooled = received[:, 0:TILE, :].astype(jnp.float32)
    pooled = jnp.where(tile_row == 0, (pooled + tails) * (1.0 / SHORTEN), pooled)
    values = pooled.reshape(rows, size).astype(jnp.bfloat16)
    pooled = values.astype(jnp.float32)
    q = (pooled * gain_q).astype(jnp.bfloat16)
    k = (pooled * gain_k).astype(jnp.bfloat16)
    incoming_f = received[:, 2 * TILE : 3 * TILE, :].astype(jnp.float32).reshape(rows, size)
    incoming = incoming_f.astype(jnp.bfloat16)
    k_pos, q_pos = iotas(rows, rows)
    scores = jnp.where(k_pos <= q_pos, mm_nt(k, q) * temper, NEGATIVE)
    weights = jnp.exp(scores - jnp.max(scores, axis=0, keepdims=True))
    weights = weights * (1.0 / jnp.sum(weights, axis=0, keepdims=True))
    grads = mm_nt(values, incoming)
    dots = jnp.sum(weights * grads, axis=0, keepdims=True)
    ds = (weights * (grads - dots)).astype(jnp.bfloat16)
    grad_q = mm_tn(ds, k) * temper
    grad_k = mm(ds, q) * temper
    grad_v = mm(weights.astype(jnp.bfloat16), incoming)
    grad = incoming_f + grad_q * gain_q + grad_k * gain_k + grad_v
    sum_q = jnp.sum(grad_q * pooled, axis=0, keepdims=True)
    sum_k = jnp.sum(grad_k * pooled, axis=0, keepdims=True)
    gain = jnp.where(copy == 0, sum_q, sum_k)
    gain_high = gain.astype(jnp.bfloat16).astype(jnp.float32)
    gain_low = gain - gain_high
    half = TILE // COPIES
    grad = grad.reshape(count, TILE, size)
    following = jnp.concatenate([grad[1:, 0:1, :], jnp.zeros((1, 1, size), jnp.float32)], axis=0)
    later = jnp.where(tile_row == half, following, jnp.roll(grad, -half, axis=1))
    block = jnp.where(copy == 0, grad, later)
    block = jnp.where(tile_row == half + 1, gain_high[None], block)
    block = jnp.where(tile_row == half + 2, gain_low[None], block)
    block = jnp.where(tile_row == half + 3, 0.0, block)
    send[...] = block.astype(jnp.bfloat16)


def backward_kernel(
    tokens,
    prior,
    grad_output,
    query_gain,
    key_gain,
    weights,
    received,
    returned,
    partial,
    send,
    sums,
):
    rows, width = tokens.shape
    size = width // HEADS
    temper = size ** (-0.5)
    half = TILE // COPIES
    row, column = iotas(rows, 2 * TILE)
    short = (row + SHORTEN - 1) // SHORTEN
    short = jnp.where(short > half, short + (TILE - half), short)
    spread = jnp.where(short == column, 1.0 / SHORTEN, 0.0).astype(jnp.bfloat16)

    def work(head):
        part = slice(head * size, (head + 1) * size)
        grad_pooled = received[head * COPIES : (head + 1) * COPIES].reshape(2 * TILE, size)
        grad_mixed = grad_output[:, part].astype(jnp.float32) + mm(spread, grad_pooled)
        incoming = grad_mixed.astype(jnp.bfloat16)
        partial[:, part] = grad_mixed
        yield
        context = jnp.concatenate([prior[:, part], tokens[:, part]], axis=0)
        dw = mm_nt(context, incoming)
        yield
        w_low = weights[head]
        w = w_low.astype(jnp.float32)
        dots = jnp.sum(w * dw, axis=0, keepdims=True)
        yield
        ds = (w * (dw - dots)).astype(jnp.bfloat16)
        context_f = context.astype(jnp.float32)
        x = context_f[rows:]
        k = (context_f * key_gain[:, part]).astype(jnp.bfloat16)
        q = x * query_gain[:, part]
        scaled_q = (q * (key_gain[:, part] * temper)).astype(jnp.bfloat16)
        yield
        pair = mm_tn(ds, jnp.concatenate([k, context], axis=1))
        grad_kv = mm(
            jnp.concatenate([ds, w_low], axis=1), jnp.concatenate([scaled_q, incoming], axis=0)
        )
        yield
        grad_q, mixed_k = pair[:, :size], pair[:, size:]
        returned[:, part] = grad_kv[:rows].astype(jnp.bfloat16)
        partial[:, part] += grad_q * (query_gain[:, part] * temper) + grad_kv[rows:]
        sums[head : head + 1, :] = jnp.sum(grad_q * x, axis=0, keepdims=True)
        sums[HEADS + head : HEADS + head + 1, :] = jnp.sum(mixed_k * q, axis=0, keepdims=True)

    staggered(work)
    block = (sums[...] * temper).astype(jnp.bfloat16)
    for device in range(send.shape[0]):
        send[device] = block


def final_kernel(partial, arriving, received, short, grad_tokens, gain_grads, *, scale):
    size = received.shape[-1]
    half = TILE // COPIES
    grad_tokens[...] = (partial[...] + arriving[...].astype(jnp.float32)).astype(jnp.bfloat16)
    sums = jnp.sum(received[...].astype(jnp.float32), axis=0) * scale
    for head in range(HEADS):
        part = slice(head * size, (head + 1) * size)
        gain_grads[0:1, part] = sums[head : head + 1]
        gain_grads[1:2, part] = sums[HEADS + head : HEADS + head + 1]
        for copy in range(COPIES):
            block = short[head * COPIES + copy].astype(jnp.float32)
            total = block[half + 1 : half + 2] + block[half + 2 : half + 3]
            gain_grads[2 + copy : 3 + copy, part] = total * scale


def call(kernel, outputs, flops, scratch=()):
    return pl.pallas_call(
        kernel,
        out_shape=outputs,
        scratch_shapes=list(scratch),
        compiler_params=pltpu.CompilerParams(vmem_limit_bytes=24 << 20),
        cost_estimate=pl.CostEstimate(flops=flops, bytes_accessed=1 << 20, transcendentals=1 << 19),
    )


def exchange(value):
    return lax.all_to_all(value, CHAIN, split_axis=0, concat_axis=0, tiled=True)


def head_shards(tokens, grad_output, query_gain, key_gain, short_query_gain, short_key_gain):
    rows, width = tokens.shape
    size = width // HEADS
    count = lax.axis_size(CHAIN)
    array = jax.ShapeDtypeStruct
    low, full = jnp.bfloat16, jnp.float32
    product = 2 * rows * rows * width
    query_gain, key_gain, short_query_gain, short_key_gain = (
        gain.reshape(1, width)
        for gain in (query_gain, key_gain, short_query_gain, short_key_gain)
    )
    prior = shifted_2(tokens, CHAIN, 1)
    own_weights, peak, total, queries, grad_short = call(
        own_kernel,
        [
            array((HEADS, rows, rows), full),
            array((HEADS, rows), full),
            array((HEADS, rows), full),
            array((rows, width), low),
            array((HEADS, rows // SHORTEN, size), low),
        ],
        product,
    )(tokens, grad_output, query_gain, key_gain)
    send, weights = call(
        prior_kernel,
        [array((count, 3 * TILE, size), low), array((HEADS, 2 * rows, rows), low)],
        3 * product,
    )(tokens, prior, key_gain, queries, own_weights, peak, total, grad_short)
    back = call(short_kernel, array((count, TILE, size), low), 10 * (count * TILE) ** 2 * size)(
        exchange(send), short_query_gain, short_key_gain
    )
    back = exchange(back)
    returned, partial, sums = call(
        backward_kernel,
        [
            array((rows, width), low),
            array((rows, width), full),
            array((count, 2 * HEADS, size), low),
        ],
        8 * product,
        [pltpu.VMEM((2 * HEADS, size), full)],
    )(tokens, prior, grad_output, query_gain, key_gain, weights, back)
    arriving = shifted_2(returned, CHAIN, -1)
    sums = exchange(sums)
    return call(
        functools.partial(final_kernel, scale=(rows * count) ** (-0.5)),
        [array((rows, width), low), array((4, width), full)],
        0,
    )(partial, arriving, sums, back)


def head_scores(queries, key_rows):
    temper = queries.shape[-1] ** (-0.5)
    return (
        jnp.einsum("qhe,khe->hqk", queries, key_rows, preferred_element_type=jnp.float32) * temper
    )


def short_order(absolute, block_rows, group_rows, seq_count):
    within = absolute % group_rows
    source = absolute // group_rows
    return (within // block_rows * seq_count + source) * block_rows + within % block_rows


def shards(tokens, grad_output, query_gain, key_gain, short_query_gain, short_key_gain):
    local_rows, model_width = tokens.shape
    head_size = model_width // HEADS
    temper = head_size ** (-0.5)
    chain_index = lax.axis_index(("grp", "seq"))
    token_f = tokens.astype(jnp.float32)
    query_heads = (token_f * query_gain).astype(jnp.bfloat16).reshape(local_rows, HEADS, head_size)
    prior_rows = shifted_2(tokens, ("grp", "seq"), 1)
    context = jnp.concatenate([prior_rows, tokens], axis=0)
    context_f = context.astype(jnp.float32)
    key_heads = (
        (context_f * key_gain).astype(jnp.bfloat16).reshape(local_rows + WINDOW, HEADS, head_size)
    )
    value_heads = context.reshape(local_rows + WINDOW, HEADS, head_size)
    query_pos = chain_index * local_rows + jnp.arange(local_rows, dtype=jnp.int32)[:, None]
    key_pos = (
        chain_index * local_rows
        - WINDOW
        + jnp.arange(local_rows + WINDOW, dtype=jnp.int32)[None, :]
    )
    allowed = (key_pos <= query_pos) & (key_pos > query_pos - WINDOW) & (key_pos >= 0)
    scores = jnp.where(allowed[None], head_scores(query_heads, key_heads), NEGATIVE)
    log_total = jax.nn.logsumexp(scores, axis=-1)
    weights = jnp.where(allowed[None], jnp.exp(scores - log_total[..., None]), 0.0)
    weights_low = weights.astype(jnp.bfloat16)
    local_out = jnp.einsum(
        "hqk,khe->qhe", weights_low, value_heads, preferred_element_type=jnp.float32
    ).reshape(local_rows, model_width)
    mixed_rows = (token_f + local_out).astype(jnp.bfloat16)
    tail_rows = shifted_2(mixed_rows[local_rows - (SHORTEN - 1) :], ("grp", "seq"), 1)
    shifted = jnp.concatenate([tail_rows, mixed_rows], axis=0)[:local_rows]
    short_rows = local_rows // SHORTEN
    pooled = (
        shifted.astype(jnp.float32).reshape(short_rows, SHORTEN, model_width).sum(axis=1)
        * (1.0 / SHORTEN)
    ).astype(jnp.bfloat16)
    grad_short = (
        grad_output.astype(jnp.float32)
        .reshape(short_rows, SHORTEN, model_width)
        .sum(axis=1)
        .astype(jnp.bfloat16)
    )
    groups = lax.axis_size("grp")
    seq_count = lax.axis_size("seq")
    group_index = lax.axis_index("grp")
    seq_index = lax.axis_index("seq")
    head_width = model_width // groups
    head_part = head_width // head_size
    group_rows = short_rows * groups
    pooled_here, grad_here = (
        lax.all_to_all(
            pooled.reshape(short_rows, groups, head_width),
            "grp",
            split_axis=1,
            concat_axis=0,
            tiled=True,
        ),
        lax.all_to_all(
            grad_short.reshape(short_rows, groups, head_width),
            "grp",
            split_axis=1,
            concat_axis=0,
            tiled=True,
        ),
    )
    pooled_here = pooled_here.reshape(group_rows, head_width)
    grad_here = grad_here.reshape(group_rows, head_width)
    gain_query = lax.dynamic_slice_in_dim(short_query_gain, group_index * head_width, head_width)
    gain_key = lax.dynamic_slice_in_dim(short_key_gain, group_index * head_width, head_width)
    pooled_f = pooled_here.astype(jnp.float32)
    short_queries = (
        (pooled_f * gain_query).astype(jnp.bfloat16).reshape(group_rows, head_part, head_size)
    )
    short_keys = (
        (pooled_f * gain_key).astype(jnp.bfloat16).reshape(group_rows, head_part, head_size)
    )
    short_values = pooled_here.reshape(group_rows, head_part, head_size)
    short_incoming = grad_here.reshape(group_rows, head_part, head_size)
    own_pos = short_order(
        seq_index * group_rows + jnp.arange(group_rows, dtype=jnp.int32),
        short_rows,
        group_rows,
        seq_count,
    )
    peak = jnp.full((head_part, group_rows), NEGATIVE, jnp.float32)
    fetched_keys = lax.all_gather(short_keys, "seq", axis=0, tiled=True)
    fetched_values = lax.all_gather(short_values, "seq", axis=0, tiled=True)
    remote_pos = short_order(
        jnp.arange(fetched_keys.shape[0], dtype=jnp.int32), short_rows, group_rows, seq_count
    )
    visible = remote_pos[None, :] <= own_pos[:, None]
    piece_scores = jnp.where(visible[None], head_scores(short_queries, fetched_keys), NEGATIVE)
    highest = jnp.maximum(peak, piece_scores.max(axis=-1))
    piece_weights = jnp.where(visible[None], jnp.exp(piece_scores - highest[..., None]), 0.0)
    piece_grads = jnp.einsum(
        "qhe,khe->hqk", short_incoming, fetched_values, preferred_element_type=jnp.float32
    )
    total_sum = piece_weights.sum(axis=-1)
    weighted_sum = (piece_weights * piece_grads).sum(axis=-1)
    short_log_total = highest + jnp.log(total_sum)
    short_dot = weighted_sum / total_sum
    fetched_keys = lax.all_gather(short_keys, "seq", axis=0, tiled=True)
    fetched_values = lax.all_gather(short_values, "seq", axis=0, tiled=True)
    remote_pos = short_order(
        jnp.arange(fetched_keys.shape[0], dtype=jnp.int32), short_rows, group_rows, seq_count
    )
    visible = remote_pos[None, :] <= own_pos[:, None]
    piece_weights = jnp.where(
        visible[None],
        jnp.exp(head_scores(short_queries, fetched_keys) - short_log_total[..., None]),
        0.0,
    )
    piece_grads = jnp.einsum(
        "qhe,khe->hqk", short_incoming, fetched_values, preferred_element_type=jnp.float32
    )
    piece_ds = (piece_weights * (piece_grads - short_dot[..., None])).astype(jnp.bfloat16)
    short_gq = (
        jnp.einsum("hqk,khe->qhe", piece_ds, fetched_keys, preferred_element_type=jnp.float32)
        * temper
    )
    stats_all, dots_all = (
        lax.all_gather(short_log_total.T, "seq", axis=0, tiled=True),
        lax.all_gather(short_dot.T, "seq", axis=0, tiled=True),
    )
    fetched_queries = lax.all_gather(short_queries, "seq", axis=0, tiled=True)
    fetched_incoming = lax.all_gather(short_incoming, "seq", axis=0, tiled=True)
    count = fetched_queries.shape[0]
    remote_pos = short_order(jnp.arange(count, dtype=jnp.int32), short_rows, group_rows, seq_count)
    visible = own_pos[None, :] <= remote_pos[:, None]
    remote_total = stats_all.T
    remote_dot = dots_all.T
    piece_weights = jnp.where(
        visible[None],
        jnp.exp(head_scores(fetched_queries, short_keys) - remote_total[..., None]),
        0.0,
    )
    piece_grads = jnp.einsum(
        "qhe,khe->hqk", fetched_incoming, short_values, preferred_element_type=jnp.float32
    )
    piece_ds = (piece_weights * (piece_grads - remote_dot[..., None])).astype(jnp.bfloat16)
    grad_keys = (
        jnp.einsum("hqk,qhe->khe", piece_ds, fetched_queries, preferred_element_type=jnp.float32)
        * temper
    )
    grad_values = jnp.einsum(
        "hqk,qhe->khe",
        piece_weights.astype(jnp.bfloat16),
        fetched_incoming,
        preferred_element_type=jnp.float32,
    )
    short_gk = grad_keys
    short_gv = grad_values
    short_gq = short_gq.reshape(group_rows, head_width)
    short_gk = short_gk.reshape(group_rows, head_width)
    short_gv = short_gv.reshape(group_rows, head_width)
    grad_pooled_here = (
        grad_here.astype(jnp.float32) + short_gq * gain_query + short_gk * gain_key + short_gv
    )
    empty_width = jnp.zeros((model_width,), jnp.float32)
    grad_short_query = lax.dynamic_update_slice(
        empty_width, jnp.sum(short_gq * pooled_f, axis=0), (group_index * head_width,)
    )
    grad_short_key = lax.dynamic_update_slice(
        empty_width, jnp.sum(short_gk * pooled_f, axis=0), (group_index * head_width,)
    )
    grad_pooled = (
        lax.all_to_all(
            grad_pooled_here.reshape(group_rows, 1, head_width).astype(jnp.bfloat16),
            "grp",
            split_axis=0,
            concat_axis=1,
            tiled=True,
        )
        .astype(jnp.float32)
        .reshape(short_rows, model_width)
    )
    following = shifted_2(grad_pooled[:1], ("grp", "seq"), -1)
    grad_following = jnp.concatenate([grad_pooled[1:], following], axis=0)
    spread = jnp.concatenate(
        [
            grad_pooled[:, None],
            jnp.broadcast_to(grad_following[:, None], (short_rows, SHORTEN - 1, model_width)),
        ],
        axis=1,
    ) * (1.0 / SHORTEN)
    grad_mixed = grad_output.astype(jnp.float32) + spread.reshape(local_rows, model_width)
    incoming_heads = grad_mixed.astype(jnp.bfloat16).reshape(local_rows, HEADS, head_size)
    local_dw = jnp.einsum(
        "qhe,khe->hqk", incoming_heads, value_heads, preferred_element_type=jnp.float32
    )
    local_dot = jnp.sum(weights * local_dw, axis=-1, keepdims=True)
    local_ds = (weights * (local_dw - local_dot)).astype(jnp.bfloat16)
    local_gq = (
        jnp.einsum("hqk,khe->qhe", local_ds, key_heads, preferred_element_type=jnp.float32) * temper
    ).reshape(local_rows, model_width)
    full_gk = (
        jnp.einsum("hqk,qhe->khe", local_ds, query_heads, preferred_element_type=jnp.float32)
        * temper
    ).reshape(local_rows + WINDOW, model_width)
    full_gv = jnp.einsum(
        "hqk,qhe->khe", weights_low, incoming_heads, preferred_element_type=jnp.float32
    ).reshape(local_rows + WINDOW, model_width)
    returned = full_gk[:WINDOW] * key_gain + full_gv[:WINDOW]
    arriving = shifted_2(returned.astype(jnp.bfloat16), ("grp", "seq"), -1).astype(returned.dtype)
    edge_gain = jnp.sum(full_gk[:WINDOW] * context_f[:WINDOW], axis=0)
    local_gk = full_gk[WINDOW:]
    local_gv = full_gv[WINDOW:]
    grad_tokens = grad_mixed + local_gq * query_gain + local_gk * key_gain + local_gv
    grad_tokens = grad_tokens.at[local_rows - WINDOW :].add(arriving)
    grad_query_gain = jnp.sum(local_gq * token_f, axis=0)
    grad_key_gain = jnp.sum(local_gk * token_f, axis=0) + edge_gain
    summed = lax.psum(
        jnp.stack([grad_query_gain, grad_key_gain, grad_short_query, grad_short_key]),
        ("grp", "seq"),
    )
    total_tokens = local_rows * lax.axis_size(("grp", "seq"))
    return (grad_tokens.astype(jnp.bfloat16), summed * total_tokens ** (-0.5))


def solution(mesh):
    def program(tokens, *others):
        rows = tokens.shape[0]
        paired = mesh.size == COPIES * HEADS and rows == WINDOW == SHORTEN * TILE
        return (head_shards if paired else shards)(tokens, *others)

    return jax.shard_map(
        program,
        mesh=mesh,
        in_specs=(P(("grp", "seq"), None), P(("grp", "seq"), None), P(), P(), P(), P()),
        out_specs=(P(("grp", "seq"), None), P()),
        check_vma=False,
    )
```
